32 devices in a mesh: groups: 2 (over x), dom: 16 (over z, y, core).
Axes of the slice: x: 2, y: 2, z: 4, core: 2. Of those that a mesh axis runs over, the one named last changes fastest.
Arguments:
- points: bfloat16 [655360, 256], P(('groups', 'dom')), parts along dimension 0
- counts: int32 [32], P(('groups', 'dom')), parts along dimension 0, may hold values from 0 to 160, as said below
- destination: int32 [5120], P(('groups', 'dom')), parts along dimension 0, may hold values from -1 to 1279, as said below
- proj_weight: bfloat16 [256, 256], replicated, may hold values from -0.375 to 0.375
- proj_bias: float32 [256], replicated, may hold values from -3 to 3
- slice_weight: bfloat16 [32, 32], replicated, may hold values from -1 to 1
- softness_matrix: bfloat16 [32], replicated, may hold values from -1 to 1
- token_qkv_weight: float32 [3, 32, 32], replicated, may hold values from -1 to 1
- out_weight: bfloat16 [256, 256], replicated, may hold values from -0.375 to 0.375
- out_bias: float32 [256], replicated, may hold values from -2 to 2
Outputs:
- result: bfloat16 [327680, 256], P(('groups', 'dom')), parts along dimension 0
The draws below stay inside these ranges and needn't reach their ends.
There are 2 independent parts, one for each index of `groups`. The reference program is written for one: setup_inputs(seed, part) draws one part's arguments, and reference() takes and returns one part's arrays. A program takes and returns all parts, laid end to end along the dimension named above; an argument that names none is the same for every part. Nothing has to cross between parts.
Inputs may be any that keep to these rules, and one draw needn't show every extreme that they name: `counts`: the entries sum to 1280; each is at most 160, and some owner holds exactly 160. `destination`: slot t of owner o holds a placed tile index when t < counts[o], else -1. Placed indices of live slots are distinct and cover all 1280 placed tiles; placed tile p lies on device p // 80. At most 10 live tiles of one owner go to one device, and this is reached in every draw.
All inputs are finite; a program needn't handle non-finite values.
Results may differ from the reference program's by a relative error of at most 0.0014.
The reference program's roundings to bfloat16 on the way count: a program that leaves them out, or rounds other values in their place, can miss the bound.
Values may be sent and summed in bfloat16 or wider, within the bound.
A program may use at most 128 MiB of HBM per device.

```python
import jax
import jax.numpy as jnp
from jax import lax

MODEL_WIDTH = 256
FOCUS_GROUPS = 8
HEAD_FEATURES = 32
PARTITION_TALLY = 32
TILE = 128
LAND = 80
CAP = 160
PEER = 10
N_DOM = 16


def placement_plan(key):
    base = jax.random.fold_in(key, 7)
    slice_keys = jax.random.split(base, 5)
    order = jax.random.permutation(slice_keys[0], N_DOM)
    shifts = jax.random.randint(slice_keys[1], (N_DOM,), 0, LAND + 1)
    shifts = shifts.at[0].set(LAND).at[N_DOM - 1].set(0)
    by_place = LAND + shifts - jnp.roll(shifts, 1)
    counts = jnp.zeros((N_DOM,), jnp.int32).at[order].set(by_place.astype(jnp.int32))
    starts = jnp.cumsum(counts) - counts
    total = N_DOM * LAND
    offset = jax.random.randint(slice_keys[2], (), 0, total)
    device_order = jax.random.permutation(slice_keys[3], N_DOM)
    tile_index = jnp.arange(CAP, dtype=jnp.int32)
    scores = jax.random.randint(slice_keys[4], (N_DOM, CAP), 0, 1 << 20) * CAP + tile_index[None, :]
    live_mask = tile_index[None, :] < counts[:, None]
    scores = jnp.where(live_mask, scores, (1 << 20) * CAP + tile_index[None, :])
    ranking = jnp.argsort(jnp.argsort(scores, axis=1, stable=True), axis=1, stable=True).astype(jnp.int32)
    global_pos = (starts[:, None] + ranking + offset) % total
    placed_device = device_order[global_pos // PEER % N_DOM]
    placed_slot = global_pos // (N_DOM * PEER) * PEER + global_pos % PEER
    destination = jnp.where(live_mask, placed_device * LAND + placed_slot, -1).astype(jnp.int32)
    return (counts, destination.reshape(N_DOM * CAP))


def draw_counts(key, part):
    return placement_plan(key)[0]


def draw_destination(key, part):
    return placement_plan(key)[1]


def draw_points(key, part):
    slice_keys = jax.random.split(jax.random.fold_in(key, 11), 2)
    noise = jax.random.normal(slice_keys[0], (N_DOM * CAP, TILE, MODEL_WIDTH), jnp.float32)
    region = 0.8 * jax.random.normal(slice_keys[1], (N_DOM * CAP, 1, MODEL_WIDTH), jnp.float32)
    values = noise + region
    return values.reshape(N_DOM * CAP * TILE, MODEL_WIDTH).astype(jnp.bfloat16)


def normal_values(own_key, shape, deviation, reach, kind=jnp.bfloat16):
    return jnp.clip(deviation * jax.random.normal(own_key, shape, jnp.float32), -reach, reach).astype(kind)


def setup_inputs(seed: int = 0, part: int = 0) -> dict:
    keys = jax.random.split(jax.random.key(seed), 11)
    part_keys = jax.random.split(jax.random.fold_in(keys[10], part), 11)
    points = draw_points(jax.random.fold_in(jax.random.fold_in(keys[10], part), 71), part)
    counts = draw_counts(jax.random.fold_in(jax.random.fold_in(keys[10], part), 71), part)
    destination = draw_destination(jax.random.fold_in(jax.random.fold_in(keys[10], part), 71), part)
    proj_weight = normal_values(keys[3], (MODEL_WIDTH, MODEL_WIDTH), MODEL_WIDTH ** -0.5, 0.375)
    proj_bias = normal_values(keys[4], (MODEL_WIDTH,), 0.5, 3.0, jnp.float32)
    slice_weight = normal_values(keys[5], (HEAD_FEATURES, PARTITION_TALLY), HEAD_FEATURES ** -0.5, 1.0)
    softness_matrix = normal_values(keys[6], (HEAD_FEATURES,), HEAD_FEATURES ** -0.5, 1.0)
    token_qkv_weight = normal_values(keys[7], (3, HEAD_FEATURES, HEAD_FEATURES), HEAD_FEATURES ** -0.5, 1.0, jnp.float32)
    out_weight = normal_values(keys[8], (MODEL_WIDTH, MODEL_WIDTH), MODEL_WIDTH ** -0.5, 0.375)
    out_bias = normal_values(keys[9], (MODEL_WIDTH,), 0.3, 2.0, jnp.float32)
    return dict(points=points, counts=counts, destination=destination, proj_weight=proj_weight, proj_bias=proj_bias, slice_weight=slice_weight, softness_matrix=softness_matrix, token_qkv_weight=token_qkv_weight, out_weight=out_weight, out_bias=out_bias)


def normalize(values):
    widened = values.astype(jnp.float32)
    centred = widened - lax.optimization_barrier(jnp.mean(widened, axis=-1, keepdims=True))
    spread = lax.optimization_barrier(jnp.mean(centred * centred, axis=-1, keepdims=True))
    return (centred * lax.rsqrt(spread + 1e-05)).astype(jnp.bfloat16)

def encode(values, proj_weight, proj_bias, slice_weight, softness_matrix):
    tally_per_line = values.shape[0]
    normed = normalize(values)
    mapped_surface_vectors = (jnp.dot(normed, proj_weight, preferred_element_type=jnp.float32) + proj_bias).astype(jnp.bfloat16)
    slice_full = jnp.kron(jnp.eye(FOCUS_GROUPS, dtype=jnp.float32), slice_weight.astype(jnp.float32)).astype(jnp.bfloat16)
    softness_broadcast = jnp.kron(jnp.eye(FOCUS_GROUPS, dtype=jnp.float32), softness_matrix.astype(jnp.float32)[:, None]).astype(jnp.bfloat16)
    partition_logits = jnp.dot(mapped_surface_vectors, slice_full, preferred_element_type=jnp.float32)
    partition_softness = 0.5 + jax.nn.softplus(jnp.dot(mapped_surface_vectors, softness_broadcast, preferred_element_type=jnp.float32))
    tempered_logits = partition_logits.reshape(tally_per_line, FOCUS_GROUPS, PARTITION_TALLY) / partition_softness[:, :, None]
    raised = jnp.exp(tempered_logits)
    slice_assignment = (raised / lax.optimization_barrier(jnp.sum(raised, axis=-1, keepdims=True))).reshape(tally_per_line, FOCUS_GROUPS * PARTITION_TALLY)
    return (mapped_surface_vectors, slice_assignment.astype(jnp.bfloat16))

def partial_sums(mapped_surface_vectors, slice_assignment, live_mask):
    tally_per_line = mapped_surface_vectors.shape[0]
    masked_scores = slice_assignment * live_mask[:, None]
    numerator_sums = jnp.einsum('lzi,lzt->zit', masked_scores.reshape(tally_per_line, FOCUS_GROUPS, PARTITION_TALLY).astype(jnp.float32), mapped_surface_vectors.reshape(tally_per_line, FOCUS_GROUPS, HEAD_FEATURES).astype(jnp.float32))
    denom = lax.optimization_barrier(jnp.sum(masked_scores.astype(jnp.float32), axis=0))
    return (numerator_sums, denom)

def mix_slices(numerator_sums, denom, token_qkv_weight):
    slice_tokens = numerator_sums / (denom.reshape(FOCUS_GROUPS, PARTITION_TALLY)[:, :, None] + 1e-05)
    highest_precision = lax.Precision.HIGHEST
    slice_query = jnp.einsum('ijt,tk->ijk', slice_tokens, token_qkv_weight[0], precision=highest_precision)
    slice_keys = jnp.einsum('ijt,tk->ijk', slice_tokens, token_qkv_weight[1], precision=highest_precision)
    slice_values = jnp.einsum('ijt,tk->ijk', slice_tokens, token_qkv_weight[2], precision=highest_precision)
    scores = jnp.einsum('hme,hne->hmn', slice_query, slice_keys, precision=highest_precision) * HEAD_FEATURES ** (-0.5)
    raised = jnp.exp(scores)
    attend = raised / lax.optimization_barrier(jnp.sum(raised, axis=-1, keepdims=True))
    return jnp.einsum('hmn,hne->hme', attend, slice_values, precision=highest_precision).astype(jnp.bfloat16)

def decode(slice_assignment, mixed_tokens, out_weight, out_bias):
    tally_per_line = slice_assignment.shape[0]
    unslice_tokens = jnp.einsum('sxw,xwk->sxk', slice_assignment.reshape(tally_per_line, FOCUS_GROUPS, PARTITION_TALLY).astype(jnp.float32), mixed_tokens.astype(jnp.float32)).reshape(tally_per_line, MODEL_WIDTH).astype(jnp.bfloat16)
    return (jnp.dot(unslice_tokens, out_weight, preferred_element_type=jnp.float32) + out_bias).astype(jnp.bfloat16)

def reference(points, counts, destination, proj_weight, proj_bias, slice_weight, softness_matrix, token_qkv_weight, out_weight, out_bias):
    grouped = points.reshape(N_DOM, CAP * TILE, MODEL_WIDTH)
    row_tiles = jnp.arange(CAP * TILE, dtype=jnp.int32) // TILE
    live_all = (row_tiles[None, :] < counts[:, None]).astype(jnp.bfloat16)

    def gather_stats(pair):
        block, live_mask = pair
        mapped_surface_vectors, slice_assignment = encode(block, proj_weight, proj_bias, slice_weight, softness_matrix)
        return partial_sums(mapped_surface_vectors, slice_assignment, live_mask)
    numer_all, denom_all = lax.map(gather_stats, (grouped, live_all))
    mixed_tokens = mix_slices(lax.optimization_barrier(jnp.sum(numer_all, axis=0)), lax.optimization_barrier(jnp.sum(denom_all, axis=0)), token_qkv_weight)

    def finish(block):
        mapped_surface_vectors, slice_assignment = encode(block, proj_weight, proj_bias, slice_weight, softness_matrix)
        return decode(slice_assignment, mixed_tokens, out_weight, out_bias)
    outputs = lax.map(finish, grouped).reshape(N_DOM * CAP, TILE, MODEL_WIDTH)
    target = jnp.where(destination >= 0, destination, N_DOM * LAND).astype(jnp.int32)
    landed = jnp.zeros((N_DOM * LAND + 1, TILE, MODEL_WIDTH), outputs.dtype).at[target].set(outputs)
    return landed[:N_DOM * LAND].reshape(N_DOM * LAND * TILE, MODEL_WIDTH)
```

```python
import functools

import jax
import jax.numpy as jnp
from jax import lax
from jax.experimental import pallas as pl
from jax.experimental.pallas import tpu as pltpu
from jax.sharding import PartitionSpec as P

WIDTH = 256
HEADS = 8
FEAT = 32
TILE = 128
LAND = 80
LABEL_ROWS = 16
HALF = 128
MESH = pl.DeviceIdType.MESH
HIGHEST = lax.Precision.HIGHEST
F32 = jnp.float32
BF16 = jnp.bfloat16


def gather_kernel(n, per_peer, order, points, out, hold, in_sem, out_sem):
    def load(k, _):
        def one(t, _):
            s = k * per_peer + t
            pltpu.make_async_copy(points.at[order[s]], hold.at[s], in_sem.at[k]).start()
            return 0

        return lax.fori_loop(0, per_peer, one, 0)

    lax.fori_loop(0, n, load, 0)

    def store(k, _):
        part = pl.ds(k * per_peer, per_peer)
        pltpu.make_async_copy(points.at[pl.ds(0, per_peer)], hold.at[part], in_sem.at[k]).wait()
        pltpu.make_async_copy(hold.at[part], out.at[part], out_sem.at[k]).start()
        return 0

    lax.fori_loop(0, n, store, 0)

    def finish(k, _):
        part = pl.ds(k * per_peer, per_peer)
        pltpu.make_async_copy(hold.at[part], out.at[part], out_sem.at[k]).wait()
        return 0

    lax.fori_loop(0, n, finish, 0)


def encode_rows(x, live, wp, bp, ws, wt, ones):
    x = jnp.where(live, x.astype(F32), 0.0)
    centred = x - jnp.sum(x, axis=-1, keepdims=True) * (1.0 / WIDTH)
    spread = jnp.sum(centred * centred, axis=-1, keepdims=True) * (1.0 / WIDTH)
    normed = (centred * lax.rsqrt(spread + 1e-05)).astype(BF16)
    proj = (jnp.dot(normed, wp, preferred_element_type=F32) + bp).astype(BF16)
    logits = jnp.dot(proj, ws, preferred_element_type=F32)
    soft = jnp.dot(proj, wt, preferred_element_type=F32)
    temper = 0.5 + (jnp.maximum(soft, 0.0) + jnp.log1p(jnp.exp(-jnp.abs(soft))))
    raised = jnp.exp(logits / temper)
    total = jnp.dot(raised, ones, preferred_element_type=F32, precision=HIGHEST)
    weights = (raised / total).astype(BF16)
    return proj, weights


def move_kernel(
    n, per_peer, step_tiles, outgoing, labels, wp, bp, ws, wt, ones, weights_out, labels_out, stats_out,
    arrived, held, arrived_lab, numer, denom, sums, inbox,
    send_sem, recv_sem, lab_send, lab_recv, own_sem, w_sem, red_send, red_recv,
):
    me = lax.axis_index("dom")
    barrier = pltpu.get_barrier_semaphore()
    for k in range(1, n):
        pl.semaphore_signal(barrier, inc=1, device_id={"dom": lax.rem(me + k, n)}, device_id_type=MESH)
    pl.semaphore_wait(barrier, n - 1)

    def lab_copy(k, peer):
        return pltpu.make_async_remote_copy(
            src_ref=labels.at[peer], dst_ref=arrived_lab.at[k], send_sem=lab_send.at[k],
            recv_sem=lab_recv.at[k], device_id={"dom": peer}, device_id_type=MESH,
        )

    def tile_copy(k, peer):
        return pltpu.make_async_remote_copy(
            src_ref=outgoing.at[peer], dst_ref=arrived.at[k], send_sem=send_sem.at[k],
            recv_sem=recv_sem.at[k], device_id={"dom": peer}, device_id_type=MESH,
        )

    own = pltpu.make_async_copy(outgoing.at[me], arrived.at[0], own_sem.at[0])
    own.start()
    own_lab = pltpu.make_async_copy(labels.at[me], arrived_lab.at[0], own_sem.at[1])
    own_lab.start()
    for k in range(1, n):
        lab_copy(k, lax.rem(me + k, n)).start()
    for k in range(1, n):
        tile_copy(k, lax.rem(me + k, n)).start()

    numer[...] = jnp.zeros_like(numer)
    denom[...] = jnp.zeros_like(denom)
    rows = step_tiles * TILE

    def block(k):
        def step(s, _):
            t0 = s * step_tiles
            at = pl.ds(pl.multiple_of(t0 * TILE, TILE), rows)
            x = arrived[k, at, :]
            live = jnp.concatenate(
                [
                    jnp.broadcast_to(arrived_lab[k, pl.ds(t0 + j, 1), :][:, :1], (TILE, 1))
                    for j in range(step_tiles)
                ],
                axis=0,
            ) >= 0
            proj, weights = encode_rows(x, live, wp[...], bp[...], ws[...], wt[...], ones[...])
            weights = jnp.where(live, weights.astype(F32), 0.0).astype(BF16)
            held[k, at, :] = weights
            numer[...] += lax.dot_general(
                weights, proj, (((0,), (0,)), ((), ())), preferred_element_type=F32
            )
            denom[...] += jnp.sum(weights.astype(F32).reshape(rows // 8, 8, WIDTH), axis=0)
            return 0

        lax.fori_loop(0, per_peer // step_tiles, step, 0)
        pltpu.make_async_copy(held.at[k], weights_out.at[k], w_sem.at[k]).start()

    own.wait()
    own_lab.wait()
    block(0)

    def from_peer(k, _):
        peer = lax.rem(me + k, n)
        lab_copy(k, peer).wait_recv()
        tile_copy(k, peer).wait_recv()
        block(k)
        return 0

    lax.fori_loop(1, n, from_peer, 0)

    lane_head = lax.broadcasted_iota(jnp.int32, (FEAT, HALF), 1) // FEAT
    for a in range(2):
        acc = jnp.zeros((FEAT, HALF), F32)
        for j in range(4):
            part = numer[pl.ds((a * 4 + j) * FEAT, FEAT), pl.ds(a * HALF, HALF)]
            acc = acc + jnp.where(lane_head == j, part, 0.0)
        sums[0, pl.ds(a * FEAT, FEAT), :] = acc
        total = jnp.sum(denom[:, pl.ds(a * HALF, HALF)], axis=0, keepdims=True)
        sums[0, pl.ds(2 * FEAT + a * 8, 8), :] = jnp.broadcast_to(total, (8, HALF))

    level, bit = 0, 1
    while bit < n:
        partner = me + bit - 2 * bit * (me // bit % 2)
        swap = pltpu.make_async_remote_copy(
            src_ref=sums.at[level], dst_ref=inbox.at[level], send_sem=red_send.at[level],
            recv_sem=red_recv.at[level], device_id={"dom": partner}, device_id_type=MESH,
        )
        swap.start()
        swap.wait()
        sums[level + 1] = sums[level] + inbox[level]
        level, bit = level + 1, bit * 2
    stats_out[...] = sums[level]
    labels_out[...] = arrived_lab[...]

    def finish(k, _):
        peer = lax.rem(me + k, n)
        lab_copy(k, peer).wait_send()
        tile_copy(k, peer).wait_send()
        return 0

    lax.fori_loop(1, n, finish, 0)

    def drain(k, _):
        pltpu.make_async_copy(held.at[k], weights_out.at[k], w_sem.at[k]).wait()
        return 0

    lax.fori_loop(0, n, drain, 0)


def mix(stats, qkv, ones):
    row_head = lax.broadcasted_iota(jnp.int32, (HALF, HALF), 0) // FEAT
    lane_head = lax.broadcasted_iota(jnp.int32, (HALF, HALF), 1) // FEAT
    same = row_head == lane_head
    blocks = []
    for a in range(2):
        numer = stats[a * FEAT:(a + 1) * FEAT, :]
        row = stats[2 * FEAT + a * 8:2 * FEAT + (a + 1) * 8, :]
        col = jnp.transpose(jnp.broadcast_to(row[:1], (HALF, HALF)))
        spread = jnp.zeros((FEAT, HALF), F32)
        for j in range(4):
            spread = spread + jnp.where(
                lane_head[:FEAT] == j, col[j * FEAT:(j + 1) * FEAT, :], 0.0
            )
        tokens = numer / (spread + 1e-05)
        dot = functools.partial(jnp.dot, preferred_element_type=F32, precision=HIGHEST)
        query, keys, values = (dot(tokens, qkv[i]) for i in range(3))
        spread_keys = jnp.where(same, jnp.concatenate([keys] * 4, axis=0), 0.0)
        scores = lax.dot_general(
            query, spread_keys, (((1,), (1,)), ((), ())), preferred_element_type=F32, precision=HIGHEST
        ) * FEAT ** (-0.5)
        raised = jnp.exp(scores)
        attend = raised / dot(raised, ones)
        spread_values = jnp.where(same, jnp.concatenate([values] * 4, axis=0), 0.0)
        mixed = dot(attend, spread_values)
        blocks.append(jnp.where(same, jnp.concatenate([mixed] * 4, axis=0), 0.0))
    nil = jnp.zeros((HALF, HALF), F32)
    return jnp.concatenate(
        [jnp.concatenate([blocks[0], nil], axis=1), jnp.concatenate([nil, blocks[1]], axis=1)], axis=0
    ).astype(BF16)


def decode_kernel(
    chunks, per_chunk, chosen, weights, stats, qkv, ones, wo, bo, out, held, done, mixed, in_sem, out_sem
):
    def load(c, _):
        def one(t, _):
            p = c * per_chunk + t
            pltpu.make_async_copy(weights.at[chosen[p]], held.at[p], in_sem.at[c]).start()
            return 0

        return lax.fori_loop(0, per_chunk, one, 0)

    lax.fori_loop(0, chunks, load, 0)
    mixed[...] = mix(stats[...], qkv, ones[...])
    rows = per_chunk * TILE

    def step(c, _):
        part = pl.ds(c * per_chunk, per_chunk)
        pltpu.make_async_copy(weights.at[pl.ds(0, per_chunk)], held.at[part], in_sem.at[c]).wait()
        w = held[part].reshape(rows, WIDTH)
        deslice = jnp.dot(w, mixed[...], preferred_element_type=F32).astype(BF16)
        y = (jnp.dot(deslice, wo[...], preferred_element_type=F32) + bo[...]).astype(BF16)
        at = pl.ds(pl.multiple_of(c * rows, rows), rows)
        done[at, :] = y
        pltpu.make_async_copy(done.at[at], out.at[at], out_sem.at[c]).start()
        return 0

    lax.fori_loop(0, chunks, step, 0)

    def finish(c, _):
        at = pl.ds(pl.multiple_of(c * rows, rows), rows)
        pltpu.make_async_copy(done.at[at], out.at[at], out_sem.at[c]).wait()
        return 0

    lax.fori_loop(0, chunks, finish, 0)


def plan(destination, own_count, n):
    slots = destination.shape[0]
    per_peer = slots // n
    index = jnp.arange(slots, dtype=jnp.int32)
    live = index < own_count
    target = jnp.where(live, destination // LAND, -1)
    slot = jnp.where(live, destination % LAND, -1)
    earlier = (target[:, None] == target[None, :]) & live[None, :] & (index[None, :] < index[:, None])
    rank = jnp.sum(earlier.astype(jnp.int32), axis=1)
    place = target * per_peer + rank
    matches = live[None, :] & (place[None, :] == index[:, None])
    source = jnp.sum(jnp.where(matches, index[None, :], 0), axis=1)
    label = jnp.sum(jnp.where(matches, slot[None, :] + 1, 0), axis=1) - 1
    return source, label


def on_device(n, points, counts, destination, wp, bp, slice_weight, softness, qkv, wo, bo):
    slots = points.shape[0] // TILE
    per_peer = slots // n
    any_spec = pl.BlockSpec(memory_space=pl.ANY)
    vmem = pl.BlockSpec(memory_space=pltpu.VMEM)
    source, label = plan(destination, counts[0], n)
    outgoing = pl.pallas_call(
        functools.partial(gather_kernel, n, per_peer),
        out_shape=jax.ShapeDtypeStruct((slots, TILE, WIDTH), BF16),
        grid_spec=pltpu.PrefetchScalarGridSpec(
            num_scalar_prefetch=1, grid=(), in_specs=[any_spec], out_specs=any_spec,
            scratch_shapes=[
                pltpu.VMEM((slots, TILE, WIDTH), BF16),
                pltpu.SemaphoreType.DMA((n,)), pltpu.SemaphoreType.DMA((n,)),
            ],
        ),
        compiler_params=pltpu.CompilerParams(vmem_limit_bytes=60 << 20),
        name="gather",
    )(source, points.reshape(slots, TILE, WIDTH))

    rows = per_peer * TILE
    labels = jnp.broadcast_to(
        jnp.pad(label.reshape(n, per_peer), ((0, 0), (0, LABEL_ROWS - per_peer)), constant_values=-1)[
            :, :, None
        ],
        (n, LABEL_ROWS, HALF),
    )
    eye = jnp.eye(HEADS, dtype=F32)
    ws = jnp.kron(eye, slice_weight.astype(F32)).astype(BF16)
    wt = jnp.kron(eye, jnp.broadcast_to(softness.astype(F32)[:, None], (FEAT, FEAT))).astype(BF16)
    ones = jnp.kron(eye, jnp.ones((FEAT, FEAT), F32))
    step_tiles = 2 if per_peer % 2 == 0 else 1
    levels = (n - 1).bit_length()
    stat_rows = 2 * FEAT + 16
    weights, arrived_lab, stats = pl.pallas_call(
        functools.partial(move_kernel, n, per_peer, step_tiles),
        out_shape=(
            jax.ShapeDtypeStruct((n, rows, WIDTH), BF16),
            jax.ShapeDtypeStruct((n, LABEL_ROWS, HALF), jnp.int32),
            jax.ShapeDtypeStruct((stat_rows, HALF), F32),
        ),
        in_specs=[any_spec, any_spec] + [vmem] * 5,
        out_specs=(any_spec, vmem, vmem),
        scratch_shapes=[
            pltpu.VMEM((n, rows, WIDTH), BF16),
            pltpu.VMEM((n, rows, WIDTH), BF16),
            pltpu.VMEM((n, LABEL_ROWS, HALF), jnp.int32),
            pltpu.VMEM((WIDTH, WIDTH), F32),
            pltpu.VMEM((8, WIDTH), F32),
            pltpu.VMEM((levels + 1, stat_rows, HALF), F32),
            pltpu.VMEM((levels, stat_rows, HALF), F32),
            pltpu.SemaphoreType.DMA((n,)), pltpu.SemaphoreType.DMA((n,)),
            pltpu.SemaphoreType.DMA((n,)), pltpu.SemaphoreType.DMA((n,)),
            pltpu.SemaphoreType.DMA((2,)), pltpu.SemaphoreType.DMA((n,)),
            pltpu.SemaphoreType.DMA((levels,)), pltpu.SemaphoreType.DMA((levels,)),
        ],
        compiler_params=pltpu.CompilerParams(
            collective_id=0, has_side_effects=True, vmem_limit_bytes=60 << 20
        ),
        name="move",
    )(outgoing.reshape(n, rows, WIDTH), labels, wp, bp.reshape(1, WIDTH), ws, wt, ones)

    slot_label = arrived_lab[:, :per_peer, 0].reshape(slots)
    index = jnp.arange(slots, dtype=jnp.int32)
    picks = slot_label[None, :] == jnp.arange(LAND, dtype=jnp.int32)[:, None]
    chosen = jnp.sum(jnp.where(picks, index[None, :], 0), axis=1)
    qkv_wide = jax.vmap(lambda w: jnp.kron(jnp.eye(4, dtype=F32), w))(qkv)
    per_chunk = 8
    chunks = LAND // per_chunk
    return pl.pallas_call(
        functools.partial(decode_kernel, chunks, per_chunk),
        out_shape=jax.ShapeDtypeStruct((LAND * TILE, WIDTH), BF16),
        grid_spec=pltpu.PrefetchScalarGridSpec(
            num_scalar_prefetch=1, grid=(), in_specs=[any_spec] + [vmem] * 5, out_specs=any_spec,
            scratch_shapes=[
                pltpu.VMEM((LAND, TILE, WIDTH), BF16),
                pltpu.VMEM((LAND * TILE, WIDTH), BF16),
                pltpu.VMEM((WIDTH, WIDTH), BF16),
                pltpu.SemaphoreType.DMA((chunks,)), pltpu.SemaphoreType.DMA((chunks,)),
            ],
        ),
        compiler_params=pltpu.CompilerParams(vmem_limit_bytes=60 << 20),
        name="decode",
    )(
        chosen, weights.reshape(slots, TILE, WIDTH), stats, qkv_wide, ones[:HALF, :HALF], wo,
        bo.reshape(1, WIDTH),
    )


def solution(mesh):
    spec = P(("groups", "dom"))
    wide = P(("groups", "dom"), None)
    return jax.shard_map(
        functools.partial(on_device, mesh.shape["dom"]),
        mesh=mesh,
        in_specs=(wide, spec, spec) + (P(),) * 7,
        out_specs=wide,
        check_vma=False,
    )
```

```python
import functools

import jax
import jax.numpy as jnp
from jax import lax
from jax.experimental import pallas as pl
from jax.experimental.pallas import tpu as pltpu
from jax.sharding import PartitionSpec as P

WIDTH = 256
HEADS = 8
FEAT = 32
TILE = 128
LAND = 80
HALF = 128
MESH = pl.DeviceIdType.MESH
HIGHEST = lax.Precision.HIGHEST
F32 = jnp.float32
BF16 = jnp.bfloat16


def split(x):
    high = x.astype(BF16)
    return high, x - high.astype(F32)


def encode_rows(x, wp, bp, ws, wt, spread_ones, ones):
    x = x.astype(F32)
    centred = x - jnp.sum(x, axis=-1, keepdims=True) * (1.0 / WIDTH)
    spread = jnp.sum(centred * centred, axis=-1, keepdims=True) * (1.0 / WIDTH)
    normed = (centred * lax.rsqrt(spread + 1e-05)).astype(BF16)
    dot = functools.partial(jnp.dot, preferred_element_type=F32)
    proj = (dot(normed, wp) + bp).astype(BF16)
    logits = dot(proj, ws)
    soft = dot(proj, wt)
    temper = 0.5 + (jnp.maximum(soft, 0.0) + jnp.log1p(jnp.exp(-jnp.abs(soft))))
    first, rest = split(1.0 / temper)
    second, rest = split(rest)
    scale = dot(first, spread_ones) + (dot(second, spread_ones) + dot(rest.astype(BF16), spread_ones))
    raised = jnp.exp(logits * scale)
    first, rest = split(raised)
    total = dot(first, ones) + dot(rest.astype(BF16), ones)
    return proj, (raised / total).astype(BF16)


def move_kernel(
    n, per_peer, unit, source, label, points, labels, wp, bp, ws, wt, spread_ones, ones, head_ones, qkv,
    wo, bo, result, labels_out,
    held_points, sending, arrived, numer, denom, sums, inbox, mixed,
    point_sem, send_sem, recv_sem, lab_send, lab_recv, own_sem, out_sem, red_send, red_recv,
):
    me = lax.axis_index("dom")
    pieces = per_peer // unit
    rows = unit * TILE
    fetch = pltpu.make_async_copy(points, held_points, point_sem)
    fetch.start()

    def partner(x):
        peer, bit = 0, 1
        while bit < n:
            mine, flip = me // bit % 2, x // bit % 2
            peer = peer + bit * (mine + flip - 2 * mine * flip)
            bit = bit * 2
        return peer

    barrier = pltpu.get_barrier_semaphore()
    for x in range(1, n):
        pl.semaphore_signal(barrier, inc=1, device_id={"dom": partner(x)}, device_id_type=MESH)
    numer[...] = jnp.zeros_like(numer)
    denom[...] = jnp.zeros_like(denom)
    pl.semaphore_wait(barrier, n - 1)

    def lab_copy(x):
        peer = partner(x)
        return pltpu.make_async_remote_copy(
            src_ref=labels.at[peer], dst_ref=labels_out.at[me], send_sem=lab_send.at[x],
            recv_sem=lab_recv.at[x], device_id={"dom": peer}, device_id_type=MESH,
        )

    def piece_copy(x, s):
        at = pl.ds(pl.multiple_of(s * rows, rows), rows)
        return pltpu.make_async_remote_copy(
            src_ref=sending.at[x, at], dst_ref=arrived.at[x, at], send_sem=send_sem.at[x, s],
            recv_sem=recv_sem.at[x, s], device_id={"dom": partner(x)}, device_id_type=MESH,
        )

    def lab_start(x, _):
        lab_copy(x).start()
        return 0

    lax.fori_loop(1, n, lab_start, 0)
    own_lab = pltpu.make_async_copy(labels.at[me], labels_out.at[me], own_sem)
    own_lab.start()
    fetch.wait()

    def compute(x, peer, s):
        first = peer * per_peer + s * unit
        tiles = jnp.concatenate([held_points[source[first + j]] for j in range(unit)], axis=0)
        proj, weights = encode_rows(
            tiles, wp[...], bp[...], ws[...], wt[...], spread_ones[...], ones[...]
        )
        live = jnp.concatenate(
            [jnp.full((TILE, WIDTH), label[first + j], jnp.int32) for j in range(unit)], axis=0
        ) >= 0
        kept = jnp.where(live, weights.astype(F32), 0.0)
        weights = kept.astype(BF16)
        sending[x, pl.ds(pl.multiple_of(s * rows, rows), rows), :] = weights
        numer[...] += lax.dot_general(
            weights, proj, (((0,), (0,)), ((), ())), preferred_element_type=F32
        )
        denom[...] += jnp.sum(kept.reshape(rows // 8, 8, WIDTH), axis=0)

    steps = (n - 1) * pieces

    def encode_step(i, _):
        x = n - 1 - i // pieces
        compute(x, partner(x), i % pieces)

        @pl.when(i > 0)
        def _():
            piece_copy(n - 1 - (i - 1) // pieces, (i - 1) % pieces).start()

        return 0

    lax.fori_loop(0, steps, encode_step, 0)

    def own_step(s, _):
        compute(0, me, s)

        @pl.when(s == 0)
        def _():
            piece_copy(1, pieces - 1).start()

        return 0

    lax.fori_loop(0, pieces, own_step, 0)

    lane_head = lax.broadcasted_iota(jnp.int32, (FEAT, HALF), 1) // FEAT
    for a in range(2):
        acc = jnp.zeros((FEAT, HALF), F32)
        for j in range(4):
            part = numer[pl.ds((a * 4 + j) * FEAT, FEAT), pl.ds(a * HALF, HALF)]
            acc = acc + jnp.where(lane_head == j, part, 0.0)
        sums[0, pl.ds(a * FEAT, FEAT), :] = acc
        total = jnp.sum(denom[:, pl.ds(a * HALF, HALF)], axis=0, keepdims=True)
        sums[0, pl.ds(2 * FEAT + a * 8, 8), :] = jnp.broadcast_to(total, (8, HALF))

    level, bit = 0, 1
    while bit < n:
        swap = pltpu.make_async_remote_copy(
            src_ref=sums.at[level], dst_ref=inbox.at[level], send_sem=red_send.at[level],
            recv_sem=red_recv.at[level], device_id={"dom": partner(bit)}, device_id_type=MESH,
        )
        swap.start()
        swap.wait()
        sums[level + 1] = sums[level] + inbox[level]
        level, bit = level + 1, bit * 2
    mixed[...] = mix(sums[level], qkv, head_ones[...])

    def decode(read, x):
        def one(s, _):
            at = pl.ds(pl.multiple_of(s * rows, rows), rows)
            deslice = jnp.dot(read[x, at, :], mixed[...], preferred_element_type=F32).astype(BF16)
            y = (jnp.dot(deslice, wo[...], preferred_element_type=F32) + bo[...]).astype(BF16)
            arrived[x, at, :] = y
            return 0

        lax.fori_loop(0, pieces, one, 0)
        pltpu.make_async_copy(arrived.at[x], result.at[partner(x)], out_sem.at[x]).start()

    decode(sending, 0)

    def from_peer(i, _):
        x = n - 1 - i

        def one(s, _):
            piece_copy(x, s).wait_recv()
            return 0

        lax.fori_loop(0, pieces, one, 0)
        decode(arrived, x)
        return 0

    lax.fori_loop(0, n - 1, from_peer, 0)

    def finish(x, _):
        def one(s, _):
            piece_copy(x, s).wait_send()
            return 0

        lax.fori_loop(0, pieces, one, 0)
        lab_copy(x).wait()
        return 0

    lax.fori_loop(1, n, finish, 0)
    own_lab.wait()

    def drain(x, _):
        pltpu.make_async_copy(arrived.at[x], result.at[partner(x)], out_sem.at[x]).wait()
        return 0

    lax.fori_loop(0, n, drain, 0)


def mix(stats, qkv, ones):
    row_head = lax.broadcasted_iota(jnp.int32, (HALF, HALF), 0) // FEAT
    lane_head = lax.broadcasted_iota(jnp.int32, (HALF, HALF), 1) // FEAT
    same = row_head == lane_head
    blocks = []
    for a in range(2):
        numer = stats[a * FEAT:(a + 1) * FEAT, :]
        row = stats[2 * FEAT + a * 8:2 * FEAT + (a + 1) * 8, :]
        col = jnp.transpose(jnp.broadcast_to(row[:1], (HALF, HALF)))
        spread = jnp.zeros((FEAT, HALF), F32)
        for j in range(4):
            spread = spread + jnp.where(
                lane_head[:FEAT] == j, col[j * FEAT:(j + 1) * FEAT, :], 0.0
            )
        tokens = numer / (spread + 1e-05)
        dot = functools.partial(jnp.dot, preferred_element_type=F32, precision=HIGHEST)
        query, keys, values = (dot(tokens, qkv[i]) for i in range(3))
        spread_keys = jnp.where(same, jnp.concatenate([keys] * 4, axis=0), 0.0)
        scores = lax.dot_general(
            query, spread_keys, (((1,), (1,)), ((), ())), preferred_element_type=F32, precision=HIGHEST
        ) * FEAT ** (-0.5)
        raised = jnp.exp(scores)
        attend = raised / dot(raised, ones)
        spread_values = jnp.where(same, jnp.concatenate([values] * 4, axis=0), 0.0)
        mixed = dot(attend, spread_values)
        blocks.append(jnp.where(same, jnp.concatenate([mixed] * 4, axis=0), 0.0))
    nil = jnp.zeros((HALF, HALF), F32)
    return jnp.concatenate(
        [jnp.concatenate([blocks[0], nil], axis=1), jnp.concatenate([nil, blocks[1]], axis=1)], axis=0
    ).astype(BF16)


def place_kernel(n, per_peer, chunks, per_chunk, labels, tiles, out, held, in_sem, out_sem):
    def load(k, _):
        def one(t, _):
            slot = labels[k, t]

            @pl.when(slot >= 0)
            def _():
                pltpu.make_async_copy(
                    tiles.at[k * per_peer + t], held.at[slot], in_sem.at[slot // per_chunk]
                ).start()

            return 0

        return lax.fori_loop(0, per_peer, one, 0)

    lax.fori_loop(0, n, load, 0)

    def step(c, _):
        part = pl.ds(c * per_chunk, per_chunk)
        pltpu.make_async_copy(tiles.at[pl.ds(0, per_chunk)], held.at[part], in_sem.at[c]).wait()
        pltpu.make_async_copy(held.at[part], out.at[part], out_sem.at[c]).start()
        return 0

    lax.fori_loop(0, chunks, step, 0)

    def finish(c, _):
        part = pl.ds(c * per_chunk, per_chunk)
        pltpu.make_async_copy(held.at[part], out.at[part], out_sem.at[c]).wait()
        return 0

    lax.fori_loop(0, chunks, finish, 0)


def plan(destination, own_count, n):
    slots = destination.shape[0]
    per_peer = slots // n
    index = jnp.arange(slots, dtype=jnp.int32)
    live = index < own_count
    target = jnp.where(live, destination // LAND, -1)
    slot = jnp.where(live, destination % LAND, -1)
    earlier = (target[:, None] == target[None, :]) & live[None, :] & (index[None, :] < index[:, None])
    rank = jnp.sum(earlier.astype(jnp.int32), axis=1)
    place = target * per_peer + rank
    matches = live[None, :] & (place[None, :] == index[:, None])
    source = jnp.sum(jnp.where(matches, index[None, :], 0), axis=1)
    label = jnp.sum(jnp.where(matches, slot[None, :] + 1, 0), axis=1) - 1
    return source, label


def on_device(n, points, counts, destination, wp, bp, slice_weight, softness, qkv, wo, bo):
    slots = points.shape[0] // TILE
    per_peer = slots // n
    any_spec = pl.BlockSpec(memory_space=pl.ANY)
    vmem = pl.BlockSpec(memory_space=pltpu.VMEM)
    smem = pl.BlockSpec(memory_space=pltpu.SMEM)
    source, label = plan(destination, counts[0], n)
    rows = per_peer * TILE
    labels = jnp.pad(label.reshape(n, 1, per_peer), ((0, 0), (0, 0), (0, HALF - per_peer)))
    eye = jnp.eye(HEADS, dtype=F32)
    ws = jnp.kron(eye, slice_weight.astype(F32)).astype(BF16)
    narrow = jnp.eye(HEADS, HALF, dtype=F32)
    wt = jnp.kron(narrow, softness.astype(F32)[:, None])
    wt = wt.reshape(WIDTH, HALF).astype(BF16)
    spread_ones = jnp.kron(narrow, jnp.ones((FEAT, 1), F32)).reshape(WIDTH, HALF).T.astype(BF16)
    ones = jnp.kron(eye, jnp.ones((FEAT, FEAT), F32))
    qkv_wide = jax.vmap(lambda w: jnp.kron(jnp.eye(4, dtype=F32), w))(qkv)
    unit = 2 if per_peer % 2 == 0 else 1
    pieces = per_peer // unit
    levels = (n - 1).bit_length()
    stat_rows = 2 * FEAT + 16
    dma = pltpu.SemaphoreType.DMA
    tiles, arrived_lab = pl.pallas_call(
        functools.partial(move_kernel, n, per_peer, unit),
        out_shape=(
            jax.ShapeDtypeStruct((n, rows, WIDTH), BF16),
            jax.ShapeDtypeStruct((n, 1, HALF), jnp.int32),
        ),
        in_specs=[smem, smem, any_spec, any_spec] + [vmem] * 10,
        out_specs=(any_spec, any_spec),
        scratch_shapes=[
            pltpu.VMEM((slots, TILE, WIDTH), BF16),
            pltpu.VMEM((n, rows, WIDTH), BF16),
            pltpu.VMEM((n, rows, WIDTH), BF16),
            pltpu.VMEM((WIDTH, WIDTH), F32),
            pltpu.VMEM((8, WIDTH), F32),
            pltpu.VMEM((levels + 1, stat_rows, HALF), F32),
            pltpu.VMEM((levels, stat_rows, HALF), F32),
            pltpu.VMEM((WIDTH, WIDTH), BF16),
            dma, dma((n, pieces)), dma((n, pieces)), dma((n,)), dma((n,)), dma, dma((n,)),
            dma((levels,)), dma((levels,)),
        ],
        compiler_params=pltpu.CompilerParams(
            collective_id=0, has_side_effects=True, vmem_limit_bytes=60 << 20
        ),
        name="move",
    )(
        source, label, points.reshape(slots, TILE, WIDTH), labels, wp, bp.reshape(1, WIDTH), ws, wt,
        spread_ones, ones.astype(BF16), ones[:HALF, :HALF], qkv_wide, wo, bo.reshape(1, WIDTH),
    )

    per_chunk = 8
    chunks = LAND // per_chunk
    placed = pl.pallas_call(
        functools.partial(place_kernel, n, per_peer, chunks, per_chunk),
        out_shape=jax.ShapeDtypeStruct((LAND, TILE, WIDTH), BF16),
        grid_spec=pltpu.PrefetchScalarGridSpec(
            num_scalar_prefetch=1, grid=(), in_specs=[any_spec], out_specs=any_spec,
            scratch_shapes=[pltpu.VMEM((LAND, TILE, WIDTH), BF16), dma((chunks,)), dma((chunks,))],
        ),
        compiler_params=pltpu.CompilerParams(vmem_limit_bytes=60 << 20),
        name="place",
    )(arrived_lab.reshape(n, HALF), tiles.reshape(slots, TILE, WIDTH))
    return placed.reshape(LAND * TILE, WIDTH)


def solution(mesh):
    spec = P(("groups", "dom"))
    wide = P(("groups", "dom"), None)
    return jax.shard_map(
        functools.partial(on_device, mesh.shape["dom"]),
        mesh=mesh,
        in_specs=(wide, spec, spec) + (P(),) * 7,
        out_specs=wide,
        check_vma=False,
    )
```

```python
import functools

import jax
import jax.numpy as jnp
from jax import lax
from jax.experimental import pallas as pl
from jax.experimental.pallas import tpu as pltpu
from jax.sharding import PartitionSpec as P

WIDTH = 256
HEADS = 8
FEAT = 32
TILE = 128
LAND = 80
HALF = 128
MESH = pl.DeviceIdType.MESH
HIGHEST = lax.Precision.HIGHEST
F32 = jnp.float32
BF16 = jnp.bfloat16


def split(x):
    high = x.astype(BF16)
    return high, x - high.astype(F32)


def encode_rows(x, wp, bp, ws, wt, spread_ones, ones):
    x = x.astype(F32)
    centred = x - jnp.sum(x, axis=-1, keepdims=True) * (1.0 / WIDTH)
    spread = jnp.sum(centred * centred, axis=-1, keepdims=True) * (1.0 / WIDTH)
    normed = (centred * lax.rsqrt(spread + 1e-05)).astype(BF16)
    dot = functools.partial(jnp.dot, preferred_element_type=F32)
    proj = (dot(normed, wp) + bp).astype(BF16)
    logits = dot(proj, ws)
    soft = dot(proj, wt)
    temper = 0.5 + (jnp.maximum(soft, 0.0) + jnp.log1p(jnp.exp(-jnp.abs(soft))))
    first, rest = split(1.0 / temper)
    second, rest = split(rest)
    scale = dot(first, spread_ones) + (dot(second, spread_ones) + dot(rest.astype(BF16), spread_ones))
    raised = jnp.exp(logits * scale)
    first, rest = split(raised)
    total = dot(first, ones) + dot(rest.astype(BF16), ones)
    return proj, (raised / total).astype(BF16)


def diagonal(block, times):
    wide = jnp.concatenate([block] * times, axis=1)
    full = jnp.concatenate([wide] * times, axis=0)
    size = times * FEAT
    row = lax.broadcasted_iota(jnp.int32, (size, size), 0) // FEAT
    lane = lax.broadcasted_iota(jnp.int32, (size, size), 1) // FEAT
    return jnp.where(row == lane, full, 0.0)


def build(slice_weight, softness, qkv_small, ws, wt, spread_ones, ones, head_ones, qkv):
    ws[...] = diagonal(slice_weight[...].astype(F32), HEADS).astype(BF16)
    for i in range(3):
        qkv[i] = diagonal(qkv_small[i], 4)
    unity = jnp.ones((FEAT, FEAT), F32)
    ones[...] = diagonal(unity, HEADS).astype(BF16)
    head_ones[...] = diagonal(unity, 4)
    row = lax.broadcasted_iota(jnp.int32, (HALF, WIDTH), 0)
    lane = lax.broadcasted_iota(jnp.int32, (HALF, WIDTH), 1) // FEAT
    spread_ones[...] = jnp.where(row == lane, 1.0, 0.0).astype(BF16)
    flat = jnp.concatenate([softness[...].astype(F32)] * 4, axis=1)
    tall = jnp.transpose(jnp.broadcast_to(flat, (HALF, HALF)))
    tall = jnp.concatenate([tall, tall], axis=0)
    row = lax.broadcasted_iota(jnp.int32, (WIDTH, HALF), 0) // FEAT
    lane = lax.broadcasted_iota(jnp.int32, (WIDTH, HALF), 1)
    wt[...] = jnp.where(row == lane, tall, 0.0).astype(BF16)


def move_kernel(
    n, per_peer, unit, source, label, points, labels, wp, bp, slice_weight, softness, qkv_small,
    wo, bo, result, labels_out,
    held_points, sending, arrived, numer, denom, sums, inbox, mixed,
    ws, wt, spread_ones, ones, head_ones, qkv,
    point_sem, send_sem, recv_sem, lab_send, lab_recv, own_sem, out_sem, red_send, red_recv,
):
    me = lax.axis_index("dom")
    pieces = per_peer // unit
    rows = unit * TILE
    fetch = pltpu.make_async_copy(points, held_points, point_sem)
    fetch.start()

    def partner(x):
        peer, bit = 0, 1
        while bit < n:
            mine, flip = me // bit % 2, x // bit % 2
            peer = peer + bit * (mine + flip - 2 * mine * flip)
            bit = bit * 2
        return peer

    barrier = pltpu.get_barrier_semaphore()
    for x in range(1, n):
        pl.semaphore_signal(barrier, inc=1, device_id={"dom": partner(x)}, device_id_type=MESH)
    numer[...] = jnp.zeros_like(numer)
    denom[...] = jnp.zeros_like(denom)
    build(slice_weight, softness, qkv_small, ws, wt, spread_ones, ones, head_ones, qkv)
    pl.semaphore_wait(barrier, n - 1)

    def order(i):
        quarter = n // 4
        near = lax.rem(i, 2) * 2 * quarter
        early = 3 * quarter + i // 2 - near
        late = jnp.where(i < 3 * quarter, i, n - 1 - i)
        return jnp.where(i < 2 * quarter, early, late)

    def lab_copy(x):
        peer = partner(x)
        return pltpu.make_async_remote_copy(
            src_ref=labels.at[peer], dst_ref=labels_out.at[me], send_sem=lab_send.at[x],
            recv_sem=lab_recv.at[x], device_id={"dom": peer}, device_id_type=MESH,
        )

    def piece_copy(x, s):
        at = pl.ds(pl.multiple_of(s * rows, rows), rows)
        return pltpu.make_async_remote_copy(
            src_ref=sending.at[x, at], dst_ref=arrived.at[x, at], send_sem=send_sem.at[x, s],
            recv_sem=recv_sem.at[x, s], device_id={"dom": partner(x)}, device_id_type=MESH,
        )

    def lab_start(x, _):
        lab_copy(x).start()
        return 0

    lax.fori_loop(1, n, lab_start, 0)
    own_lab = pltpu.make_async_copy(labels.at[me], labels_out.at[me], own_sem)
    own_lab.start()
    fetch.wait()

    def compute(x, peer, s):
        first = peer * per_peer + s * unit
        tiles = jnp.concatenate([held_points[source[first + j]] for j in range(unit)], axis=0)
        proj, weights = encode_rows(
            tiles, wp[...], bp[...], ws[...], wt[...], spread_ones[...], ones[...]
        )
        live = jnp.concatenate(
            [jnp.full((TILE, WIDTH), label[first + j], jnp.int32) for j in range(unit)], axis=0
        ) >= 0
        kept = jnp.where(live, weights.astype(F32), 0.0)
        weights = kept.astype(BF16)
        sending[x, pl.ds(pl.multiple_of(s * rows, rows), rows), :] = weights
        numer[...] += lax.dot_general(
            weights, proj, (((0,), (0,)), ((), ())), preferred_element_type=F32
        )
        denom[...] += jnp.sum(kept.reshape(rows // 8, 8, WIDTH), axis=0)

    steps = (n - 1) * pieces
    held_from = (n - 1) * (pieces - 1)

    def encode_step(i, _):
        x = order(i % (n - 1))
        compute(x, partner(x), i // (n - 1))

        @pl.when((i > 0) & (i <= held_from))
        def _():
            piece_copy(order((i - 1) % (n - 1)), (i - 1) // (n - 1)).start()

        return 0

    lax.fori_loop(0, steps, encode_step, 0)

    def own_step(s, _):
        compute(0, me, s)
        return 0

    lax.fori_loop(0, pieces, own_step, 0)

    lane_head = lax.broadcasted_iota(jnp.int32, (FEAT, HALF), 1) // FEAT
    for a in range(2):
        acc = jnp.zeros((FEAT, HALF), F32)
        for j in range(4):
            part = numer[pl.ds((a * 4 + j) * FEAT, FEAT), pl.ds(a * HALF, HALF)]
            acc = acc + jnp.where(lane_head == j, part, 0.0)
        sums[0, pl.ds(a * FEAT, FEAT), :] = acc
        total = jnp.sum(denom[:, pl.ds(a * HALF, HALF)], axis=0, keepdims=True)
        sums[0, pl.ds(2 * FEAT + a * 8, 8), :] = jnp.broadcast_to(total, (8, HALF))

    def release(i, _):
        piece_copy(order(i - held_from), pieces - 1).start()
        return 0

    level, bit = 0, n // 2
    while bit > 0:
        swap = pltpu.make_async_remote_copy(
            src_ref=sums.at[level], dst_ref=inbox.at[level], send_sem=red_send.at[level],
            recv_sem=red_recv.at[level], device_id={"dom": partner(bit)}, device_id_type=MESH,
        )
        swap.start()
        swap.wait()
        sums[level + 1] = sums[level] + inbox[level]
        level, bit = level + 1, bit // 2
        if level == max(1, (n - 1).bit_length() - 2):
            lax.fori_loop(held_from, steps, release, 0)
    mixed[...] = mix(sums[level], qkv, head_ones[...])

    def out_copy(x, s):
        at = pl.ds(pl.multiple_of(s * rows, rows), rows)
        return pltpu.make_async_copy(arrived.at[x, at], result.at[partner(x), at], out_sem.at[x, s])

    def decode(read, x, s):
        at = pl.ds(pl.multiple_of(s * rows, rows), rows)
        deslice = jnp.dot(read[x, at, :], mixed[...], preferred_element_type=F32).astype(BF16)
        y = (jnp.dot(deslice, wo[...], preferred_element_type=F32) + bo[...]).astype(BF16)
        arrived[x, at, :] = y
        out_copy(x, s).start()

    def decode_own(s, _):
        decode(sending, 0, s)
        return 0

    lax.fori_loop(0, pieces, decode_own, 0)

    def from_peer(i, _):
        x, s = order(i % (n - 1)), i // (n - 1)
        piece_copy(x, s).wait_recv()
        decode(arrived, x, s)
        return 0

    lax.fori_loop(0, steps, from_peer, 0)

    def finish(x, _):
        def one(s, _):
            piece_copy(x, s).wait_send()
            return 0

        lax.fori_loop(0, pieces, one, 0)
        lab_copy(x).wait()
        return 0

    lax.fori_loop(1, n, finish, 0)
    own_lab.wait()

    def drain(i, _):
        out_copy(i // pieces, i % pieces).wait()
        return 0

    lax.fori_loop(0, n * pieces, drain, 0)


def mix(stats, qkv, ones):
    row_head = lax.broadcasted_iota(jnp.int32, (HALF, HALF), 0) // FEAT
    lane_head = lax.broadcasted_iota(jnp.int32, (HALF, HALF), 1) // FEAT
    same = row_head == lane_head
    blocks = []
    for a in range(2):
        numer = stats[a * FEAT:(a + 1) * FEAT, :]
        row = stats[2 * FEAT + a * 8:2 * FEAT + (a + 1) * 8, :]
        col = jnp.transpose(jnp.broadcast_to(row[:1], (HALF, HALF)))
        spread = jnp.zeros((FEAT, HALF), F32)
        for j in range(4):
            spread = spread + jnp.where(
                lane_head[:FEAT] == j, col[j * FEAT:(j + 1) * FEAT, :], 0.0
            )
        tokens = numer / (spread + 1e-05)
        dot = functools.partial(jnp.dot, preferred_element_type=F32, precision=HIGHEST)
        query, keys, values = (dot(tokens, qkv[i]) for i in range(3))
        spread_keys = jnp.where(same, jnp.concatenate([keys] * 4, axis=0), 0.0)
        scores = lax.dot_general(
            query, spread_keys, (((1,), (1,)), ((), ())), preferred_element_type=F32, precision=HIGHEST
        ) * FEAT ** (-0.5)
        raised = jnp.exp(scores)
        attend = raised / dot(raised, ones)
        spread_values = jnp.where(same, jnp.concatenate([values] * 4, axis=0), 0.0)
        mixed = dot(attend, spread_values)
        blocks.append(jnp.where(same, jnp.concatenate([mixed] * 4, axis=0), 0.0))
    nil = jnp.zeros((HALF, HALF), F32)
    return jnp.concatenate(
        [jnp.concatenate([blocks[0], nil], axis=1), jnp.concatenate([nil, blocks[1]], axis=1)], axis=0
    ).astype(BF16)


def place_kernel(n, per_peer, chunks, per_chunk, labels, tiles, out, held, in_sem, out_sem):
    def load(k, _):
        def one(t, _):
            slot = labels[k, t]

            @pl.when(slot >= 0)
            def _():
                pltpu.make_async_copy(
                    tiles.at[k * per_peer + t], held.at[slot], in_sem.at[slot // per_chunk]
                ).start()

            return 0

        return lax.fori_loop(0, per_peer, one, 0)

    lax.fori_loop(0, n, load, 0)

    def step(c, _):
        part = pl.ds(c * per_chunk, per_chunk)
        pltpu.make_async_copy(tiles.at[pl.ds(0, per_chunk)], held.at[part], in_sem.at[c]).wait()
        pltpu.make_async_copy(held.at[part], out.at[part], out_sem.at[c]).start()
        return 0

    lax.fori_loop(0, chunks, step, 0)

    def finish(c, _):
        part = pl.ds(c * per_chunk, per_chunk)
        pltpu.make_async_copy(held.at[part], out.at[part], out_sem.at[c]).wait()
        return 0

    lax.fori_loop(0, chunks, finish, 0)


def plan(destination, own_count, n):
    slots = destination.shape[0]
    per_peer = slots // n
    index = jnp.arange(slots, dtype=jnp.int32)
    live = index < own_count
    target = jnp.where(live, destination // LAND, -1)
    slot = jnp.where(live, destination % LAND, -1)
    earlier = (target[:, None] == target[None, :]) & live[None, :] & (index[None, :] < index[:, None])
    rank = jnp.sum(earlier.astype(jnp.int32), axis=1)
    place = target * per_peer + rank
    matches = live[None, :] & (place[None, :] == index[:, None])
    source = jnp.sum(jnp.where(matches, index[None, :], 0), axis=1)
    label = jnp.sum(jnp.where(matches, slot[None, :] + 1, 0), axis=1) - 1
    return source, label


def on_device(n, points, counts, destination, wp, bp, slice_weight, softness, qkv, wo, bo):
    slots = points.shape[0] // TILE
    per_peer = slots // n
    any_spec = pl.BlockSpec(memory_space=pl.ANY)
    vmem = pl.BlockSpec(memory_space=pltpu.VMEM)
    smem = pl.BlockSpec(memory_space=pltpu.SMEM)
    source, label = plan(destination, counts[0], n)
    rows = per_peer * TILE
    labels = jnp.pad(label.reshape(n, 1, per_peer), ((0, 0), (0, 0), (0, HALF - per_peer)))
    unit = 2 if per_peer % 2 == 0 else 1
    pieces = per_peer // unit
    levels = (n - 1).bit_length()
    stat_rows = 2 * FEAT + 16
    dma = pltpu.SemaphoreType.DMA
    tiles, arrived_lab = pl.pallas_call(
        functools.partial(move_kernel, n, per_peer, unit),
        out_shape=(
            jax.ShapeDtypeStruct((n, rows, WIDTH), BF16),
            jax.ShapeDtypeStruct((n, 1, HALF), jnp.int32),
        ),
        in_specs=[smem, smem, any_spec, any_spec] + [vmem] * 7,
        out_specs=(any_spec, any_spec),
        scratch_shapes=[
            pltpu.VMEM((slots, TILE, WIDTH), BF16),
            pltpu.VMEM((n, rows, WIDTH), BF16),
            pltpu.VMEM((n, rows, WIDTH), BF16),
            pltpu.VMEM((WIDTH, WIDTH), F32),
            pltpu.VMEM((8, WIDTH), F32),
            pltpu.VMEM((levels + 1, stat_rows, HALF), F32),
            pltpu.VMEM((levels, stat_rows, HALF), F32),
            pltpu.VMEM((WIDTH, WIDTH), BF16),
            pltpu.VMEM((WIDTH, WIDTH), BF16),
            pltpu.VMEM((WIDTH, HALF), BF16),
            pltpu.VMEM((HALF, WIDTH), BF16),
            pltpu.VMEM((WIDTH, WIDTH), BF16),
            pltpu.VMEM((HALF, HALF), F32),
            pltpu.VMEM((3, HALF, HALF), F32),
            dma, dma((n, pieces)), dma((n, pieces)), dma((n,)), dma((n,)), dma, dma((n, pieces)),
            dma((levels,)), dma((levels,)),
        ],
        compiler_params=pltpu.CompilerParams(
            collective_id=0, has_side_effects=True, vmem_limit_bytes=60 << 20
        ),
        name="move",
    )(
        source, label, points.reshape(slots, TILE, WIDTH), labels, wp, bp.reshape(1, WIDTH),
        slice_weight, softness.reshape(1, FEAT), qkv, wo, bo.reshape(1, WIDTH),
    )

    per_chunk = 8
    chunks = LAND // per_chunk
    placed = pl.pallas_call(
        functools.partial(place_kernel, n, per_peer, chunks, per_chunk),
        out_shape=jax.ShapeDtypeStruct((LAND, TILE, WIDTH), BF16),
        grid_spec=pltpu.PrefetchScalarGridSpec(
            num_scalar_prefetch=1, grid=(), in_specs=[any_spec], out_specs=any_spec,
            scratch_shapes=[pltpu.VMEM((LAND, TILE, WIDTH), BF16), dma((chunks,)), dma((chunks,))],
        ),
        compiler_params=pltpu.CompilerParams(vmem_limit_bytes=60 << 20),
        name="place",
    )(arrived_lab.reshape(n, HALF), tiles.reshape(slots, TILE, WIDTH))
    return placed.reshape(LAND * TILE, WIDTH)


def solution(mesh):
    spec = P(("groups", "dom"))
    wide = P(("groups", "dom"), None)
    return jax.shard_map(
        functools.partial(on_device, mesh.shape["dom"]),
        mesh=mesh,
        in_specs=(wide, spec, spec) + (P(),) * 7,
        out_specs=wide,
        check_vma=False,
    )
```

```python
import functools

import jax
import jax.numpy as jnp
from jax import lax
from jax.experimental import pallas as pl
from jax.experimental.pallas import tpu as pltpu
from jax.sharding import PartitionSpec as P

WIDTH = 256
HEADS = 8
FEAT = 32
TILE = 128
LAND = 80
HALF = 128
MESH = pl.DeviceIdType.MESH
HIGHEST = lax.Precision.HIGHEST
F32 = jnp.float32
BF16 = jnp.bfloat16


def split(x):
    high = x.astype(BF16)
    return high, x - high.astype(F32)


def encode_rows(x, wp, bp, ws, wt, spread_ones, ones):
    x = x.astype(F32)
    centred = x - jnp.sum(x, axis=-1, keepdims=True) * (1.0 / WIDTH)
    spread = jnp.sum(centred * centred, axis=-1, keepdims=True) * (1.0 / WIDTH)
    normed = (centred * lax.rsqrt(spread + 1e-05)).astype(BF16)
    dot = functools.partial(jnp.dot, preferred_element_type=F32)
    proj = (dot(normed, wp) + bp).astype(BF16)
    logits = dot(proj, ws)
    soft = dot(proj, wt)
    temper = 0.5 + (jnp.maximum(soft, 0.0) + jnp.log1p(jnp.exp(-jnp.abs(soft))))
    first, rest = split(1.0 / temper)
    second, rest = split(rest)
    scale = dot(first, spread_ones) + (dot(second, spread_ones) + dot(rest.astype(BF16), spread_ones))
    raised = jnp.exp(logits * scale)
    first, rest = split(raised)
    total = dot(first, ones) + dot(rest.astype(BF16), ones)
    return proj, (raised / total).astype(BF16)


def diagonal(block, times):
    wide = jnp.concatenate([block] * times, axis=1)
    full = jnp.concatenate([wide] * times, axis=0)
    size = times * FEAT
    row = lax.broadcasted_iota(jnp.int32, (size, size), 0) // FEAT
    lane = lax.broadcasted_iota(jnp.int32, (size, size), 1) // FEAT
    return jnp.where(row == lane, full, 0.0)


def build(slice_weight, softness, qkv_small, ws, wt, spread_ones, ones, head_ones, qkv):
    ws[...] = diagonal(slice_weight[...].astype(F32), HEADS).astype(BF16)
    for i in range(3):
        qkv[i] = diagonal(qkv_small[i], 4)
    unity = jnp.ones((FEAT, FEAT), F32)
    ones[...] = diagonal(unity, HEADS).astype(BF16)
    head_ones[...] = diagonal(unity, 4)
    row = lax.broadcasted_iota(jnp.int32, (HALF, WIDTH), 0)
    lane = lax.broadcasted_iota(jnp.int32, (HALF, WIDTH), 1) // FEAT
    spread_ones[...] = jnp.where(row == lane, 1.0, 0.0).astype(BF16)
    flat = jnp.concatenate([softness[...].astype(F32)] * 4, axis=1)
    tall = jnp.transpose(jnp.broadcast_to(flat, (HALF, HALF)))
    tall = jnp.concatenate([tall, tall], axis=0)
    row = lax.broadcasted_iota(jnp.int32, (WIDTH, HALF), 0) // FEAT
    lane = lax.broadcasted_iota(jnp.int32, (WIDTH, HALF), 1)
    wt[...] = jnp.where(row == lane, tall, 0.0).astype(BF16)


def move_kernel(
    n, per_peer, unit, source, label, points, labels, wp, bp, slice_weight, softness, qkv_small,
    wo, bo, result, labels_out,
    held_points, sending, arrived, numer, denom, sums, inbox, mixed,
    ws, wt, spread_ones, ones, head_ones, qkv,
    point_sem, send_sem, recv_sem, lab_send, lab_recv, own_sem, out_sem, red_send, red_recv,
):
    me = lax.axis_index("dom")
    pieces = per_peer // unit
    rows = unit * TILE
    fetch = pltpu.make_async_copy(points, held_points, point_sem)
    fetch.start()

    def partner(x):
        peer, bit = 0, 1
        while bit < n:
            mine, flip = me // bit % 2, x // bit % 2
            peer = peer + bit * (mine + flip - 2 * mine * flip)
            bit = bit * 2
        return peer

    barrier = pltpu.get_barrier_semaphore()
    for x in range(1, n):
        pl.semaphore_signal(barrier, inc=1, device_id={"dom": partner(x)}, device_id_type=MESH)
    numer[...] = jnp.zeros_like(numer)
    denom[...] = jnp.zeros_like(denom)
    build(slice_weight, softness, qkv_small, ws, wt, spread_ones, ones, head_ones, qkv)
    pl.semaphore_wait(barrier, n - 1)

    def order(i):
        quarter = n // 4
        near = lax.rem(i, 2) * 2 * quarter
        early = 3 * quarter + i // 2 - near
        late = jnp.where(i < 3 * quarter, i, n - 1 - i)
        return jnp.where(i < 2 * quarter, early, late)

    def lab_copy(x):
        peer = partner(x)
        return pltpu.make_async_remote_copy(
            src_ref=labels.at[peer], dst_ref=labels_out.at[me], send_sem=lab_send.at[x],
            recv_sem=lab_recv.at[x], device_id={"dom": peer}, device_id_type=MESH,
        )

    def piece_copy(x, s):
        at = pl.ds(pl.multiple_of(s * rows, rows), rows)
        return pltpu.make_async_remote_copy(
            src_ref=sending.at[x, at], dst_ref=arrived.at[x, at], send_sem=send_sem.at[x, s],
            recv_sem=recv_sem.at[x, s], device_id={"dom": partner(x)}, device_id_type=MESH,
        )

    def lab_start(x, _):
        lab_copy(x).start()
        return 0

    lax.fori_loop(1, n, lab_start, 0)
    own_lab = pltpu.make_async_copy(labels.at[me], labels_out.at[me], own_sem)
    own_lab.start()
    fetch.wait()

    def compute(x, peer, s):
        first = peer * per_peer + s * unit
        tiles = jnp.concatenate([held_points[source[first + j]] for j in range(unit)], axis=0)
        proj, weights = encode_rows(
            tiles, wp[...], bp[...], ws[...], wt[...], spread_ones[...], ones[...]
        )
        live = jnp.concatenate(
            [jnp.full((TILE, WIDTH), label[first + j], jnp.int32) for j in range(unit)], axis=0
        ) >= 0
        kept = jnp.where(live, weights.astype(F32), 0.0)
        weights = kept.astype(BF16)
        sending[x, pl.ds(pl.multiple_of(s * rows, rows), rows), :] = weights
        numer[...] += lax.dot_general(
            weights, proj, (((0,), (0,)), ((), ())), preferred_element_type=F32
        )
        denom[...] += jnp.sum(kept.reshape(rows // 8, 8, WIDTH), axis=0)

    steps = (n - 1) * pieces
    held_from = max(0, (n - 1) * (pieces - 1) - n // 2)

    def encode_step(i, _):
        x = order(i % (n - 1))
        compute(x, partner(x), i // (n - 1))

        @pl.when((i > 0) & (i <= held_from))
        def _():
            piece_copy(order((i - 1) % (n - 1)), (i - 1) // (n - 1)).start()

        return 0

    lax.fori_loop(0, steps, encode_step, 0)

    def own_step(s, _):
        compute(0, me, s)
        return 0

    lax.fori_loop(0, pieces, own_step, 0)

    lane_head = lax.broadcasted_iota(jnp.int32, (FEAT, HALF), 1) // FEAT
    for a in range(2):
        acc = jnp.zeros((FEAT, HALF), F32)
        for j in range(4):
            part = numer[pl.ds((a * 4 + j) * FEAT, FEAT), pl.ds(a * HALF, HALF)]
            acc = acc + jnp.where(lane_head == j, part, 0.0)
        sums[0, pl.ds(a * FEAT, FEAT), :] = acc
        total = jnp.sum(denom[:, pl.ds(a * HALF, HALF)], axis=0, keepdims=True)
        sums[0, pl.ds(2 * FEAT + a * 8, 8), :] = jnp.broadcast_to(total, (8, HALF))

    def release(i, _):
        piece_copy(order(i % (n - 1)), i // (n - 1)).start()
        return 0

    level, bit = 0, n // 2
    while bit > 0:
        swap = pltpu.make_async_remote_copy(
            src_ref=sums.at[level], dst_ref=inbox.at[level], send_sem=red_send.at[level],
            recv_sem=red_recv.at[level], device_id={"dom": partner(bit)}, device_id_type=MESH,
        )
        swap.start()
        swap.wait()
        sums[level + 1] = sums[level] + inbox[level]
        level, bit = level + 1, bit // 2
        if level == max(1, (n - 1).bit_length() - 2):
            lax.fori_loop(held_from, steps, release, 0)
    mixed[...] = mix(sums[level], qkv, head_ones[...])

    def out_copy(x, s):
        at = pl.ds(pl.multiple_of(s * rows, rows), rows)
        return pltpu.make_async_copy(arrived.at[x, at], result.at[partner(x), at], out_sem.at[x, s])

    def decode(read, x, s):
        at = pl.ds(pl.multiple_of(s * rows, rows), rows)
        deslice = jnp.dot(read[x, at, :], mixed[...], preferred_element_type=F32).astype(BF16)
        y = (jnp.dot(deslice, wo[...], preferred_element_type=F32) + bo[...]).astype(BF16)
        arrived[x, at, :] = y
        out_copy(x, s).start()

    def decode_own(s, _):
        decode(sending, 0, s)
        return 0

    lax.fori_loop(0, pieces, decode_own, 0)

    def from_peer(i, _):
        x, s = order(i % (n - 1)), i // (n - 1)
        piece_copy(x, s).wait_recv()
        decode(arrived, x, s)
        return 0

    lax.fori_loop(0, steps, from_peer, 0)

    def finish(x, _):
        def one(s, _):
            piece_copy(x, s).wait_send()
            return 0

        lax.fori_loop(0, pieces, one, 0)
        lab_copy(x).wait()
        return 0

    lax.fori_loop(1, n, finish, 0)
    own_lab.wait()

    def drain(i, _):
        out_copy(i // pieces, i % pieces).wait()
        return 0

    lax.fori_loop(0, n * pieces, drain, 0)


def mix(stats, qkv, ones):
    row_head = lax.broadcasted_iota(jnp.int32, (HALF, HALF), 0) // FEAT
    lane_head = lax.broadcasted_iota(jnp.int32, (HALF, HALF), 1) // FEAT
    same = row_head == lane_head
    blocks = []
    for a in range(2):
        numer = stats[a * FEAT:(a + 1) * FEAT, :]
        row = stats[2 * FEAT + a * 8:2 * FEAT + (a + 1) * 8, :]
        col = jnp.transpose(jnp.broadcast_to(row[:1], (HALF, HALF)))
        spread = jnp.zeros((FEAT, HALF), F32)
        for j in range(4):
            spread = spread + jnp.where(
                lane_head[:FEAT] == j, col[j * FEAT:(j + 1) * FEAT, :], 0.0
            )
        tokens = numer / (spread + 1e-05)
        dot = functools.partial(jnp.dot, preferred_element_type=F32, precision=HIGHEST)
        query, keys, values = (dot(tokens, qkv[i]) for i in range(3))
        spread_keys = jnp.where(same, jnp.concatenate([keys] * 4, axis=0), 0.0)
        scores = lax.dot_general(
            query, spread_keys, (((1,), (1,)), ((), ())), preferred_element_type=F32, precision=HIGHEST
        ) * FEAT ** (-0.5)
        raised = jnp.exp(scores)
        attend = raised / dot(raised, ones)
        spread_values = jnp.where(same, jnp.concatenate([values] * 4, axis=0), 0.0)
        mixed = dot(attend, spread_values)
        blocks.append(jnp.where(same, jnp.concatenate([mixed] * 4, axis=0), 0.0))
    nil = jnp.zeros((HALF, HALF), F32)
    return jnp.concatenate(
        [jnp.concatenate([blocks[0], nil], axis=1), jnp.concatenate([nil, blocks[1]], axis=1)], axis=0
    ).astype(BF16)


def place_kernel(n, per_peer, chunks, per_chunk, labels, tiles, out, held, in_sem, out_sem):
    def load(k, _):
        def one(t, _):
            slot = labels[k, t]

            @pl.when(slot >= 0)
            def _():
                pltpu.make_async_copy(
                    tiles.at[k * per_peer + t], held.at[slot], in_sem.at[slot // per_chunk]
                ).start()

            return 0

        return lax.fori_loop(0, per_peer, one, 0)

    lax.fori_loop(0, n, load, 0)

    def step(c, _):
        part = pl.ds(c * per_chunk, per_chunk)
        pltpu.make_async_copy(tiles.at[pl.ds(0, per_chunk)], held.at[part], in_sem.at[c]).wait()
        pltpu.make_async_copy(held.at[part], out.at[part], out_sem.at[c]).start()
        return 0

    lax.fori_loop(0, chunks, step, 0)

    def finish(c, _):
        part = pl.ds(c * per_chunk, per_chunk)
        pltpu.make_async_copy(held.at[part], out.at[part], out_sem.at[c]).wait()
        return 0

    lax.fori_loop(0, chunks, finish, 0)


def plan(destination, own_count, n):
    slots = destination.shape[0]
    per_peer = slots // n
    index = jnp.arange(slots, dtype=jnp.int32)
    live = index < own_count
    target = jnp.where(live, destination // LAND, -1)
    slot = jnp.where(live, destination % LAND, -1)
    earlier = (target[:, None] == target[None, :]) & live[None, :] & (index[None, :] < index[:, None])
    rank = jnp.sum(earlier.astype(jnp.int32), axis=1)
    place = target * per_peer + rank
    matches = live[None, :] & (place[None, :] == index[:, None])
    source = jnp.sum(jnp.where(matches, index[None, :], 0), axis=1)
    label = jnp.sum(jnp.where(matches, slot[None, :] + 1, 0), axis=1) - 1
    return source, label


def on_device(n, points, counts, destination, wp, bp, slice_weight, softness, qkv, wo, bo):
    slots = points.shape[0] // TILE
    per_peer = slots // n
    any_spec = pl.BlockSpec(memory_space=pl.ANY)
    vmem = pl.BlockSpec(memory_space=pltpu.VMEM)
    smem = pl.BlockSpec(memory_space=pltpu.SMEM)
    source, label = plan(destination, counts[0], n)
    rows = per_peer * TILE
    labels = jnp.pad(label.reshape(n, 1, per_peer), ((0, 0), (0, 0), (0, HALF - per_peer)))
    unit = 2 if per_peer % 2 == 0 else 1
    pieces = per_peer // unit
    levels = (n - 1).bit_length()
    stat_rows = 2 * FEAT + 16
    dma = pltpu.SemaphoreType.DMA
    tiles, arrived_lab = pl.pallas_call(
        functools.partial(move_kernel, n, per_peer, unit),
        out_shape=(
            jax.ShapeDtypeStruct((n, rows, WIDTH), BF16),
            jax.ShapeDtypeStruct((n, 1, HALF), jnp.int32),
        ),
        in_specs=[smem, smem, any_spec, any_spec] + [vmem] * 7,
        out_specs=(any_spec, any_spec),
        scratch_shapes=[
            pltpu.VMEM((slots, TILE, WIDTH), BF16),
            pltpu.VMEM((n, rows, WIDTH), BF16),
            pltpu.VMEM((n, rows, WIDTH), BF16),
            pltpu.VMEM((WIDTH, WIDTH), F32),
            pltpu.VMEM((8, WIDTH), F32),
            pltpu.VMEM((levels + 1, stat_rows, HALF), F32),
            pltpu.VMEM((levels, stat_rows, HALF), F32),
            pltpu.VMEM((WIDTH, WIDTH), BF16),
            pltpu.VMEM((WIDTH, WIDTH), BF16),
            pltpu.VMEM((WIDTH, HALF), BF16),
            pltpu.VMEM((HALF, WIDTH), BF16),
            pltpu.VMEM((WIDTH, WIDTH), BF16),
            pltpu.VMEM((HALF, HALF), F32),
            pltpu.VMEM((3, HALF, HALF), F32),
            dma, dma((n, pieces)), dma((n, pieces)), dma((n,)), dma((n,)), dma, dma((n, pieces)),
            dma((levels,)), dma((levels,)),
        ],
        compiler_params=pltpu.CompilerParams(
            collective_id=0, has_side_effects=True, vmem_limit_bytes=60 << 20
        ),
        name="move",
    )(
        source, label, points.reshape(slots, TILE, WIDTH), labels, wp, bp.reshape(1, WIDTH),
        slice_weight, softness.reshape(1, FEAT), qkv, wo, bo.reshape(1, WIDTH),
    )

    per_chunk = 8
    chunks = LAND // per_chunk
    placed = pl.pallas_call(
        functools.partial(place_kernel, n, per_peer, chunks, per_chunk),
        out_shape=jax.ShapeDtypeStruct((LAND, TILE, WIDTH), BF16),
        grid_spec=pltpu.PrefetchScalarGridSpec(
            num_scalar_prefetch=1, grid=(), in_specs=[any_spec], out_specs=any_spec,
            scratch_shapes=[pltpu.VMEM((LAND, TILE, WIDTH), BF16), dma((chunks,)), dma((chunks,))],
        ),
        compiler_params=pltpu.CompilerParams(vmem_limit_bytes=60 << 20),
        name="place",
    )(arrived_lab.reshape(n, HALF), tiles.reshape(slots, TILE, WIDTH))
    return placed.reshape(LAND * TILE, WIDTH)


def solution(mesh):
    spec = P(("groups", "dom"))
    wide = P(("groups", "dom"), None)
    return jax.shard_map(
        functools.partial(on_device, mesh.shape["dom"]),
        mesh=mesh,
        in_specs=(wide, spec, spec) + (P(),) * 7,
        out_specs=wide,
        check_vma=False,
    )
```
